32 devices in a mesh: rep: 4 (over x, core), own: 8 (over z, y).
Axes of the slice: x: 2, y: 2, z: 4, core: 2. Of those that a mesh axis runs over, the one named last changes fastest.
Arguments:
- weights: float32 [4, 256, 8, 2048], P('rep', 'own'), may hold values from -6 to 6
- anchor: float32 [832, 8, 2048], P('own'), may hold values from -6 to 6
- momentum: float32 [832, 8, 2048], P('own'), may hold values from -3 to 3
- owner: int32 [256], replicated, may hold values from 0 to 7, as said below
- emb_weights: float32 [4, 1024, 2048], P('rep', 'own'), may hold values from -6 to 6
- emb_anchor: float32 [1024, 2048], P('own'), may hold values from -6 to 6
- emb_momentum: float32 [1024, 2048], P('own'), may hold values from -3 to 3
- sketch: float32 [64, 2048], replicated, may hold values from -0.125 to 0.125
- inv_root: float32 [64, 64], replicated
Outputs:
- new_weights: float32 [256, 8, 2048], P('own')
- new_momentum: float32 [832, 8, 2048], P('own')
- new_embedding: float32 [1024, 2048], P('own')
- new_emb_momentum: float32 [1024, 2048], P('own')
The draws below stay inside these ranges and needn't reach their ends.
Inputs may be any that keep to these rules, and one draw needn't show every extreme that they name: Each owner holds at least 8 and at most 104 tiles, and some owner holds exactly 104. Of the 32 tiles of one aligned block, at most 13 have the same owner, and some block reaches 13.
All inputs are finite; a program needn't handle non-finite values.
Results may differ from the reference program's by a relative error of at most 0.0001.
Values sent between devices are 32-bit elements; how exact they have to be, the bound alone decides.
A program may use at most 128 MiB of HBM per device.

```python
import math
import jax
import jax.numpy as jnp
from jax import lax

D = 2048
RANK = 64
TILE_ROWS = 8
TILES_DEV = 32
HALF = 8
HOT = 2
CAP = 104
TILES = 256
SLOTS = 832
EMB = 1024
N_REP = 4
N_OWN = 8


def draw_owner(key, part):
    key_shift, key_hot = jax.random.split(key)
    shifts = jax.random.permutation(key_shift, N_OWN)[:HALF].astype(jnp.int32)
    hot_list = jax.random.permutation(key_hot, N_OWN)[:HOT].astype(jnp.int32)
    block_ids = jnp.arange(N_OWN, dtype=jnp.int32)[:, None]
    column = jnp.arange(TILES_DEV, dtype=jnp.int32)[None, :]
    spread = (block_ids + shifts[jnp.minimum(column, HALF - 1)]) % N_OWN
    crowded = hot_list[(block_ids + column) % HOT]
    return jnp.where(column < HALF, spread, crowded).reshape(-1).astype(jnp.int32)


def draw_inv_root(key, part):
    overall = 1.0 / math.sqrt(1.25 * EMB)
    jitter = jnp.clip(jax.random.normal(key, (RANK, RANK), jnp.float32), -4.0, 4.0)
    return (overall * (jnp.eye(RANK, dtype=jnp.float32) + 0.3 / math.sqrt(RANK) * jitter)).astype(jnp.float32)


def level_of(stream_key, shape, cuts, least, largest):
    gain = 1.0
    for axis_at, blocks in cuts:
        steps = jax.random.uniform(jax.random.fold_in(jax.random.fold_in(stream_key, 6), axis_at), (blocks,), jnp.float32, least / len(cuts), largest / len(cuts))
        gain = gain * jnp.repeat(jnp.exp(steps), shape[axis_at] // blocks).reshape((-1,) + (1,) * (len(shape) - 1 - axis_at))
    return gain


def scatter_about(key, extent, scale, bound, cuts=(), kind=jnp.bfloat16):
    drawn = jax.random.normal(key, extent, jnp.float32) * scale
    if len(cuts) > 0:
        drawn = level_of(key, extent, cuts, -0.22, 0.18) * drawn
    return jnp.clip(drawn, min=-bound, max=bound).astype(kind)


def setup_inputs(seed: int = 0) -> dict:
    key_of = jax.random.split(jax.random.key(seed), 10)
    return {
        "weights": scatter_about(key_of[0], (N_REP, TILES, TILE_ROWS, D), 1.0, 6.0, ((0, 4), (1, 8)), jnp.float32),
        "anchor": scatter_about(key_of[1], (SLOTS, TILE_ROWS, D), 1.0, 6.0, ((0, 8),), jnp.float32),
        "momentum": scatter_about(key_of[2], (SLOTS, TILE_ROWS, D), 0.5, 3.0, ((0, 8),), jnp.float32),
        "owner": draw_owner(jax.random.fold_in(key_of[9], 71), 0),
        "emb_weights": scatter_about(key_of[4], (N_REP, EMB, D), 1.0, 6.0, ((0, 4), (1, 8)), jnp.float32),
        "emb_anchor": scatter_about(key_of[5], (EMB, D), 1.0, 6.0, ((0, 8),), jnp.float32),
        "emb_momentum": scatter_about(key_of[6], (EMB, D), 0.5, 3.0, ((0, 8),), jnp.float32),
        "sketch": scatter_about(key_of[7], (RANK, D), D ** -0.5, 0.125, (), jnp.float32),
        "inv_root": draw_inv_root(jax.random.fold_in(key_of[9], 71), 0),
    }


OUTER_RATE = 0.7
OUTER_MOMENTUM = 0.9


def reference(weights, anchor, momentum, owner, emb_weights, emb_anchor, emb_momentum, sketch, inv_root):
    highest = lax.Precision.HIGHEST
    tile_ids = jnp.arange(owner.shape[0], dtype=jnp.int32)
    same_owner = owner[:, None] == owner[None, :]
    earlier = tile_ids[None, :] < tile_ids[:, None]
    slot_rank = jnp.sum(same_owner & earlier, axis=1).astype(jnp.int32)
    slot = (owner * CAP + slot_rank).astype(jnp.int32)
    anchor_tiles = anchor[slot]
    momentum_tiles = momentum[slot]
    weight_mean = jnp.sum(weights, axis=0) * (1.0 / N_REP)
    outer_grad = anchor_tiles - weight_mean
    moved = OUTER_MOMENTUM * momentum_tiles + outer_grad
    new_weights = anchor_tiles - OUTER_RATE * (outer_grad + OUTER_MOMENTUM * moved)
    new_momentum = jnp.zeros_like(momentum).at[slot].set(moved)
    sketch_total = jnp.zeros((RANK, EMB), jnp.float32)
    for group in range(N_REP):
        emb_diff = emb_anchor - emb_weights[group]
        sketch_total = sketch_total + lax.dot_general(sketch, emb_diff, (((1,), (1,)), ((), ())), precision=highest, preferred_element_type=jnp.float32)
    sketch_mean = sketch_total * (1.0 / N_REP)
    basis_rows = jnp.dot(inv_root, sketch_mean, precision=highest, preferred_element_type=jnp.float32)
    factor_total = jnp.zeros((RANK, D), jnp.float32)
    for group in range(N_REP):
        emb_diff = emb_anchor - emb_weights[group]
        factor_total = factor_total + jnp.dot(basis_rows, emb_diff, precision=highest, preferred_element_type=jnp.float32)
    factor = factor_total * (1.0 / N_REP)
    approx = lax.dot_general(basis_rows, factor, (((0,), (0,)), ((), ())), precision=highest, preferred_element_type=jnp.float32)
    new_emb_momentum = OUTER_MOMENTUM * emb_momentum + approx
    new_embedding = emb_anchor - OUTER_RATE * (approx + OUTER_MOMENTUM * new_emb_momentum)
    return new_weights, new_momentum, new_embedding, new_emb_momentum
```

```python
import jax
import jax.numpy as jnp
from jax import lax
from jax.sharding import PartitionSpec as P

OUTER_RATE = 0.7
OUTER_MOMENTUM = 0.9


def owner_tables(owner, tiles_dev, per_pair, capacity, own_index, own_count):
    tile_count = owner.shape[0]
    tile_ids = jnp.arange(tile_count, dtype=jnp.int32)
    block_of = tile_ids // tiles_dev
    same_owner = owner[:, None] == owner[None, :]
    earlier = tile_ids[None, :] < tile_ids[:, None]
    slot_rank = jnp.sum(same_owner & earlier, axis=1, dtype=jnp.int32)
    pair_rank = jnp.sum(
        same_owner & earlier & (block_of[:, None] == block_of[None, :]), axis=1, dtype=jnp.int32
    )
    local_owner = lax.dynamic_slice_in_dim(owner, own_index * tiles_dev, tiles_dev)
    local_pair = lax.dynamic_slice_in_dim(pair_rank, own_index * tiles_dev, tiles_dev)
    dest_ids = jnp.arange(own_count, dtype=jnp.int32)[:, None, None]
    pair_ids = jnp.arange(per_pair, dtype=jnp.int32)[None, :, None]
    outgoing_match = (local_owner[None, None, :] == dest_ids) & (
        local_pair[None, None, :] == pair_ids
    )
    local_ids = jnp.arange(tiles_dev, dtype=jnp.int32)[None, None, :]
    local_pick = jnp.sum(jnp.where(outgoing_match, local_ids, 0), axis=2).reshape(-1)
    shard_read = local_owner * per_pair + local_pair
    held_here = owner == own_index
    slot_ids = jnp.arange(capacity, dtype=jnp.int32)[:, None]
    holder_match = held_here[None, :] & (slot_rank[None, :] == slot_ids)
    owner_read = jnp.sum(
        jnp.where(holder_match, (block_of * per_pair + pair_rank)[None, :], 0), axis=1
    )
    is_filled = jnp.any(holder_match, axis=1)
    return_match = (
        held_here[None, None, :]
        & (block_of[None, None, :] == dest_ids)
        & (pair_rank[None, None, :] == pair_ids)
    )
    owner_pick = jnp.sum(jnp.where(return_match, slot_rank[None, None, :], 0), axis=2).reshape(-1)
    return (local_pick, shard_read, owner_read, is_filled, owner_pick)


def local(
    weights, anchor, momentum, owner, emb_weights, emb_anchor, emb_momentum, sketch, inv_root
):
    own_count = lax.axis_size("own")
    rep_count = lax.axis_size("rep")
    own_index = lax.axis_index("own")
    tiles_dev = weights.shape[1]
    tile_rows = weights.shape[2]
    width = weights.shape[3]
    capacity = anchor.shape[0]
    half_tiles = min(tiles_dev // 2, own_count)
    hot_count = max(own_count // 4, 1)
    per_pair = (tiles_dev - half_tiles) // hot_count + 1
    local_pick, shard_read, owner_read, is_filled, owner_pick = owner_tables(
        owner, tiles_dev, per_pair, capacity, own_index, own_count
    )
    rep_index = lax.axis_index("rep")
    part = width // rep_count
    mean_part = lax.psum_scatter(weights[0], "rep", scatter_dimension=2, tiled=True) * (
        1.0 / rep_count
    )
    anchor_part = lax.dynamic_slice_in_dim(anchor, rep_index * part, part, axis=2)
    momentum_part = lax.dynamic_slice_in_dim(momentum, rep_index * part, part, axis=2)
    held_part = anchor_part - OUTER_RATE * (
        (1.0 + OUTER_MOMENTUM) * anchor_part + OUTER_MOMENTUM * OUTER_MOMENTUM * momentum_part
    )

    def exchange(tiles, pick):
        sent = jnp.take(tiles, pick, axis=0).reshape(own_count, per_pair, tile_rows, part)
        return lax.all_to_all(sent, "own", split_axis=0, concat_axis=0, tiled=True).reshape(
            own_count * per_pair, tile_rows, part
        )

    landed = jnp.take(exchange(held_part, owner_pick), shard_read, axis=0)
    new_part = landed + OUTER_RATE * (1.0 + OUTER_MOMENTUM) * mean_part
    placed_part = jnp.take(exchange(mean_part, local_pick), owner_read, axis=0)
    new_weights = lax.all_gather(new_part, "rep", axis=2, tiled=True)
    weight_mean = lax.all_gather(placed_part, "rep", axis=2, tiled=True)
    moved = OUTER_MOMENTUM * momentum + (anchor - weight_mean)
    new_momentum = jnp.where(is_filled[:, None, None], moved, 0.0)
    highest = lax.Precision.HIGHEST
    emb_diff = emb_anchor - emb_weights[0]
    local_sketch = lax.dot_general(
        sketch,
        emb_diff,
        (((1,), (1,)), ((), ())),
        precision=highest,
        preferred_element_type=jnp.float32,
    )
    sketch_mean = lax.psum(local_sketch, "rep") * (1.0 / rep_count)
    basis_rows = jnp.dot(
        inv_root, sketch_mean, precision=highest, preferred_element_type=jnp.float32
    )
    local_factor = jnp.dot(
        basis_rows, emb_diff, precision=highest, preferred_element_type=jnp.float32
    )
    factor = lax.psum(local_factor, ("rep", "own")) * (1.0 / rep_count)
    approx = lax.dot_general(
        basis_rows,
        factor,
        (((0,), (0,)), ((), ())),
        precision=highest,
        preferred_element_type=jnp.float32,
    )
    new_emb_momentum = OUTER_MOMENTUM * emb_momentum + approx
    new_embedding = emb_anchor - OUTER_RATE * (approx + OUTER_MOMENTUM * new_emb_momentum)
    return (new_weights, new_momentum, new_embedding, new_emb_momentum)


def solution(mesh):
    placed = (
        P("rep", "own", None, None),
        P("own", None, None),
        P("own", None, None),
        P(),
        P("rep", "own", None),
        P("own", None),
        P("own", None),
        P(),
        P(),
    )
    return jax.shard_map(
        local,
        mesh=mesh,
        in_specs=placed,
        out_specs=(P("own", None, None), P("own", None, None), P("own", None), P("own", None)),
        check_vma=False,
    )
```

```python
import functools

import jax
import jax.numpy as jnp
from jax import lax
from jax.experimental import pallas as pl
from jax.experimental.pallas import tpu as pltpu
from jax.sharding import PartitionSpec as P

OUTER_RATE = 0.7
OUTER_MOMENTUM = 0.9


def owner_tables(owner, tiles_dev, per_pair, capacity, own_index, own_count):
    tile_count = owner.shape[0]
    tile_ids = jnp.arange(tile_count, dtype=jnp.int32)
    block_of = tile_ids // tiles_dev
    same_owner = owner[:, None] == owner[None, :]
    earlier = tile_ids[None, :] < tile_ids[:, None]
    slot_rank = jnp.sum(same_owner & earlier, axis=1, dtype=jnp.int32)
    pair_rank = jnp.sum(
        same_owner & earlier & (block_of[:, None] == block_of[None, :]), axis=1, dtype=jnp.int32
    )
    local_owner = lax.dynamic_slice_in_dim(owner, own_index * tiles_dev, tiles_dev)
    local_pair = lax.dynamic_slice_in_dim(pair_rank, own_index * tiles_dev, tiles_dev)
    dest_ids = jnp.arange(own_count, dtype=jnp.int32)[:, None, None]
    pair_ids = jnp.arange(per_pair, dtype=jnp.int32)[None, :, None]
    outgoing_match = (local_owner[None, None, :] == dest_ids) & (
        local_pair[None, None, :] == pair_ids
    )
    local_ids = jnp.arange(tiles_dev, dtype=jnp.int32)[None, None, :]
    local_pick = jnp.sum(jnp.where(outgoing_match, local_ids, 0), axis=2).reshape(-1)
    shard_read = local_owner * per_pair + local_pair
    held_here = owner == own_index
    slot_ids = jnp.arange(capacity, dtype=jnp.int32)[:, None]
    holder_match = held_here[None, :] & (slot_rank[None, :] == slot_ids)
    owner_read = jnp.sum(
        jnp.where(holder_match, (block_of * per_pair + pair_rank)[None, :], 0), axis=1
    )
    is_filled = jnp.any(holder_match, axis=1)
    return_match = (
        held_here[None, None, :]
        & (block_of[None, None, :] == dest_ids)
        & (pair_rank[None, None, :] == pair_ids)
    )
    owner_pick = jnp.sum(jnp.where(return_match, slot_rank[None, None, :], 0), axis=2).reshape(-1)
    return (local_pick, shard_read, owner_read, is_filled, owner_pick)


FIXED = 1.0 + OUTER_MOMENTUM
SQUARED = OUTER_MOMENTUM * OUTER_MOMENTUM


def flip(index, bits):
    out, unit = index, 1
    while unit <= bits:
        if bits & unit:
            out = out + unit - 2 * unit * ((index // unit) % 2)
        unit *= 2
    return out


def route_kernel(
    own_count, per_pair, groups,
    local_pick, shard_read, owner_read, filled, owner_pick, weights, anchor, momentum,
    new_weights, new_momentum,
    anchor_part, momentum_part, mine, core_in, chip_out, chip_in, mean, held_out, held_in,
    mean_out, gathered, fresh, anchor_all, momentum_all,
    local_sem, core_send, core_recv, chip_send, chip_recv, held_send, held_recv,
    mean_send, mean_recv, gc_send, gc_recv, gx_send, gx_recv, gf_send, gf_recv,
    fresh_send, fresh_recv, tile_sem, slot_sem,
):
    rep = lax.axis_index("rep")
    own = lax.axis_index("own")
    core_peer, chip_peer, far_peer = flip(rep, 1), flip(rep, 2), flip(rep, 3)
    tiles, part = mean.shape[0], mean.shape[2]
    slots = anchor_part.shape[0]

    def columns(index):
        return pl.ds(pl.multiple_of(index * part, 128), part)

    def to_rep(src, dst, send, recv, peer):
        return pltpu.make_async_remote_copy(
            src_ref=src, dst_ref=dst, send_sem=send, recv_sem=recv,
            device_id=(peer, own), device_id_type=pl.DeviceIdType.MESH,
        )

    def to_own(src, dst, send, recv, peer):
        return pltpu.make_async_remote_copy(
            src_ref=src, dst_ref=dst, send_sem=send, recv_sem=recv,
            device_id=(rep, peer), device_id_type=pl.DeviceIdType.MESH,
        )

    first = [
        pltpu.make_async_copy(anchor.at[:, :, columns(rep)], anchor_part, local_sem.at[0]),
        pltpu.make_async_copy(momentum.at[:, :, columns(rep)], momentum_part, local_sem.at[1]),
        pltpu.make_async_copy(weights.at[0, :, :, columns(rep)], mine.at[0], local_sem.at[2]),
        pltpu.make_async_copy(weights.at[0, :, :, columns(chip_peer)], mine.at[1], local_sem.at[3]),
    ]
    for copy in first:
        copy.start()

    barrier = pltpu.get_barrier_semaphore()
    for peer in (core_peer, chip_peer):
        pl.semaphore_signal(
            barrier, inc=1, device_id=(peer, own), device_id_type=pl.DeviceIdType.MESH
        )
    for k in range(1, own_count):
        pl.semaphore_signal(
            barrier, inc=1, device_id=(rep, flip(own, k)), device_id_type=pl.DeviceIdType.MESH
        )
    pl.semaphore_wait(barrier, own_count + 1)

    core_copies = [
        to_rep(
            weights.at[0, :, :, columns(source)], core_in.at[j], core_send.at[j],
            core_recv.at[j], core_peer,
        )
        for j, source in ((1, far_peer), (0, core_peer))
    ]
    for copy in core_copies:
        copy.start()

    first[0].wait()
    first[1].wait()
    held_copies = []
    for k in list(range(1, own_count)) + [0]:
        peer = flip(own, k)

        def fill(p, carry, k=k, peer=peer):
            slot = owner_pick[peer * per_pair + p]
            a = anchor_part[slot]
            value = a - OUTER_RATE * (FIXED * a + SQUARED * momentum_part[slot])
            if k == 0:
                held_in[own * per_pair + p] = value
            else:
                held_out[k * per_pair + p] = value
            return carry

        lax.fori_loop(0, per_pair, fill, 0)
        if k:
            copy = to_own(
                held_out.at[pl.ds(k * per_pair, per_pair)],
                held_in.at[pl.ds(own * per_pair, per_pair)],
                held_send.at[k], held_recv.at[k], peer,
            )
            copy.start()
            held_copies.append(copy)

    whole = [
        pltpu.make_async_copy(anchor, anchor_all, local_sem.at[4]),
        pltpu.make_async_copy(momentum, momentum_all, local_sem.at[5]),
    ]
    for copy in whole:
        copy.start()

    first[2].wait()
    first[3].wait()
    core_copies[0].wait_recv()

    def half_sum(t, carry):
        chip_out[t] = mine[1, t] + core_in[1, t]
        return carry

    lax.fori_loop(0, tiles, half_sum, 0)
    chip_copy = to_rep(chip_out, chip_in, chip_send.at[0], chip_recv.at[0], chip_peer)
    chip_copy.start()
    core_copies[1].wait_recv()
    chip_copy.wait_recv()

    def full_sum(t, carry):
        mean[t] = (mine[0, t] + core_in[0, t] + chip_in[t]) * 0.25
        return carry

    lax.fori_loop(0, tiles, full_sum, 0)

    mean_copies = {}
    for k in list(range(1, own_count)) + [0]:
        peer = flip(own, k)

        def fill_mean(p, carry, k=k, peer=peer):
            value = mean[local_pick[peer * per_pair + p]]
            if k == 0:
                gathered[rep, own * per_pair + p] = value
            else:
                mean_out[k * per_pair + p] = value
            return carry

        lax.fori_loop(0, per_pair, fill_mean, 0)
        if k:
            copy = to_own(
                mean_out.at[pl.ds(k * per_pair, per_pair)],
                gathered.at[rep, pl.ds(own * per_pair, per_pair)],
                mean_send.at[k], mean_recv.at[k], peer,
            )
            copy.start()
            mean_copies[k] = copy

    near, cross, passed = {}, {}, {}

    def spread(k):
        rows = pl.ds(flip(own, k) * per_pair, per_pair)
        if k:
            mean_copies[k].wait_recv()
        here = gathered.at[rep, rows]
        cross[k] = to_rep(here, here, gx_send.at[k], gx_recv.at[k], chip_peer)
        near[k] = to_rep(here, here, gc_send.at[k], gc_recv.at[k], core_peer)
        cross[k].start()
        near[k].start()

    def pass_on(k):
        rows = pl.ds(flip(own, k) * per_pair, per_pair)
        cross[k].wait_recv()
        there = gathered.at[chip_peer, rows]
        passed[k] = to_rep(there, there, gf_send.at[k], gf_recv.at[k], core_peer)
        passed[k].start()

    early = min(2, own_count)
    for k in range(early):
        spread(k)

    for copy in held_copies:
        copy.wait_recv()

    def renew(t, carry):
        fresh[rep, t] = held_in[shard_read[t]] + (OUTER_RATE * FIXED) * mean[t]
        return carry

    lax.fori_loop(0, tiles, renew, 0)
    fresh_copies = [
        to_rep(fresh.at[rep], fresh.at[rep], fresh_send.at[0], fresh_recv.at[0], chip_peer),
        to_rep(fresh.at[rep], fresh.at[rep], fresh_send.at[1], fresh_recv.at[1], core_peer),
    ]
    for copy in fresh_copies:
        copy.start()

    for k in range(early, own_count):
        spread(k)
        pass_on(k - early)
    fresh_copies[0].wait_recv()
    last = to_rep(
        fresh.at[chip_peer], fresh.at[chip_peer], fresh_send.at[2], fresh_recv.at[2], core_peer
    )
    last.start()
    fresh_copies.append(last)
    for k in range(own_count - early, own_count):
        pass_on(k)

    fresh_copies[1].wait_recv()
    last.wait_recv()
    tile_copies = [
        pltpu.make_async_copy(
            fresh.at[q], new_weights.at[:, :, pl.ds(q * part, part)], tile_sem.at[q]
        )
        for q in range(4)
    ]
    for copy in tile_copies:
        copy.start()
    for copy in whole:
        copy.wait()
    for k in range(own_count):
        near[k].wait_recv()
        passed[k].wait_recv()

    size = slots // groups
    slot_copies = []
    for g in range(groups):

        def advance(j, carry, g=g):
            s = g * size + j
            row = owner_read[s]
            kept = jnp.full((8, 128), filled[s], jnp.int32) > 0
            kept = jnp.concatenate([kept.astype(jnp.float32)] * (part // 128), axis=1) > 0.5
            for q in range(4):
                at = pl.ds(q * part, part)
                moved = OUTER_MOMENTUM * momentum_all[s, :, at] + (
                    anchor_all[s, :, at] - gathered[q, row]
                )
                momentum_all[s, :, at] = jnp.where(kept, moved, 0.0)
            return carry

        lax.fori_loop(0, size, advance, 0)
        copy = pltpu.make_async_copy(
            momentum_all.at[pl.ds(g * size, size)],
            new_momentum.at[pl.ds(g * size, size)],
            slot_sem.at[g],
        )
        copy.start()
        slot_copies.append(copy)

    for copy in core_copies + [chip_copy] + held_copies + fresh_copies:
        copy.wait_send()
    for k in range(own_count):
        if k:
            mean_copies[k].wait_send()
        near[k].wait_send()
        cross[k].wait_send()
        passed[k].wait_send()
    for copy in tile_copies + slot_copies:
        copy.wait()


def route(weights, anchor, momentum, tables, own_count, per_pair):
    tiles, rows, width = weights.shape[1:]
    slots, part = anchor.shape[0], width // 4
    pairs = own_count * per_pair
    groups = 8 if slots % 8 == 0 else 1
    f32, dma = jnp.float32, pltpu.SemaphoreType.DMA
    scratch = [
        pltpu.VMEM((slots, rows, part), f32), pltpu.VMEM((slots, rows, part), f32),
        pltpu.VMEM((2, tiles, rows, part), f32), pltpu.VMEM((2, tiles, rows, part), f32),
        pltpu.VMEM((tiles, rows, part), f32), pltpu.VMEM((tiles, rows, part), f32),
        pltpu.VMEM((tiles, rows, part), f32),
        pltpu.VMEM((pairs, rows, part), f32), pltpu.VMEM((pairs, rows, part), f32),
        pltpu.VMEM((pairs, rows, part), f32), pltpu.VMEM((4, pairs, rows, part), f32),
        pltpu.VMEM((4, tiles, rows, part), f32),
        pltpu.VMEM((slots, rows, width), f32), pltpu.VMEM((slots, rows, width), f32),
        dma((6,)), dma((2,)), dma((2,)), dma((1,)), dma((1,)),
    ] + [dma((own_count,)) for _ in range(10)] + [dma((3,)), dma((3,)), dma((4,)), dma((groups,))]
    return pl.pallas_call(
        functools.partial(route_kernel, own_count, per_pair, groups),
        out_shape=(
            jax.ShapeDtypeStruct((tiles, rows, width), f32),
            jax.ShapeDtypeStruct((slots, rows, width), f32),
        ),
        in_specs=[pl.BlockSpec(memory_space=pltpu.SMEM)] * 5 + [pl.BlockSpec(memory_space=pl.ANY)] * 3,
        out_specs=(pl.BlockSpec(memory_space=pl.ANY), pl.BlockSpec(memory_space=pl.ANY)),
        scratch_shapes=scratch,
        compiler_params=pltpu.CompilerParams(
            collective_id=0, has_side_effects=True, vmem_limit_bytes=60 * 1024 * 1024
        ),
        cost_estimate=pl.CostEstimate(flops=20000000, bytes_accessed=300000000, transcendentals=0),
    )(*tables, weights, anchor, momentum)


def local(
    weights, anchor, momentum, owner, emb_weights, emb_anchor, emb_momentum, sketch, inv_root
):
    own_count = lax.axis_size("own")
    rep_count = lax.axis_size("rep")
    own_index = lax.axis_index("own")
    tiles_dev = weights.shape[1]
    capacity = anchor.shape[0]
    half_tiles = min(tiles_dev // 2, own_count)
    hot_count = max(own_count // 4, 1)
    per_pair = (tiles_dev - half_tiles) // hot_count + 1
    local_pick, shard_read, owner_read, is_filled, owner_pick = owner_tables(
        owner, tiles_dev, per_pair, capacity, own_index, own_count
    )
    tables = (local_pick, shard_read, owner_read, is_filled.astype(jnp.int32), owner_pick)
    new_weights, new_momentum = route(weights, anchor, momentum, tables, own_count, per_pair)
    highest = lax.Precision.HIGHEST
    emb_diff = emb_anchor - emb_weights[0]
    local_sketch = lax.dot_general(
        sketch,
        emb_diff,
        (((1,), (1,)), ((), ())),
        precision=highest,
        preferred_element_type=jnp.float32,
    )
    sketch_mean = lax.psum(local_sketch, "rep") * (1.0 / rep_count)
    basis_rows = jnp.dot(
        inv_root, sketch_mean, precision=highest, preferred_element_type=jnp.float32
    )
    local_factor = jnp.dot(
        basis_rows, emb_diff, precision=highest, preferred_element_type=jnp.float32
    )
    factor = lax.psum(local_factor, ("rep", "own")) * (1.0 / rep_count)
    approx = lax.dot_general(
        basis_rows,
        factor,
        (((0,), (0,)), ((), ())),
        precision=highest,
        preferred_element_type=jnp.float32,
    )
    new_emb_momentum = OUTER_MOMENTUM * emb_momentum + approx
    new_embedding = emb_anchor - OUTER_RATE * (approx + OUTER_MOMENTUM * new_emb_momentum)
    return (new_weights, new_momentum, new_embedding, new_emb_momentum)


def solution(mesh):
    placed = (
        P("rep", "own", None, None),
        P("own", None, None),
        P("own", None, None),
        P(),
        P("rep", "own", None),
        P("own", None),
        P("own", None),
        P(),
        P(),
    )
    return jax.shard_map(
        local,
        mesh=mesh,
        in_specs=placed,
        out_specs=(P("own", None, None), P("own", None, None), P("own", None), P("own", None)),
        check_vma=False,
    )
```

```python
import functools

import jax
import jax.numpy as jnp
from jax import lax
from jax.experimental import pallas as pl
from jax.experimental.pallas import tpu as pltpu
from jax.sharding import PartitionSpec as P

OUTER_RATE = 0.7
OUTER_MOMENTUM = 0.9


def owner_tables(owner, tiles_dev, per_pair, capacity, own_index, own_count):
    tile_count = owner.shape[0]
    tile_ids = jnp.arange(tile_count, dtype=jnp.int32)
    block_of = tile_ids // tiles_dev
    same_owner = owner[:, None] == owner[None, :]
    earlier = tile_ids[None, :] < tile_ids[:, None]
    slot_rank = jnp.sum(same_owner & earlier, axis=1, dtype=jnp.int32)
    pair_rank = jnp.sum(
        same_owner & earlier & (block_of[:, None] == block_of[None, :]), axis=1, dtype=jnp.int32
    )
    local_owner = lax.dynamic_slice_in_dim(owner, own_index * tiles_dev, tiles_dev)
    local_pair = lax.dynamic_slice_in_dim(pair_rank, own_index * tiles_dev, tiles_dev)
    dest_ids = jnp.arange(own_count, dtype=jnp.int32)[:, None, None]
    pair_ids = jnp.arange(per_pair, dtype=jnp.int32)[None, :, None]
    outgoing_match = (local_owner[None, None, :] == dest_ids) & (
        local_pair[None, None, :] == pair_ids
    )
    local_ids = jnp.arange(tiles_dev, dtype=jnp.int32)[None, None, :]
    local_pick = jnp.sum(jnp.where(outgoing_match, local_ids, 0), axis=2).reshape(-1)
    shard_read = local_owner * per_pair + local_pair
    held_here = owner == own_index
    slot_ids = jnp.arange(capacity, dtype=jnp.int32)[:, None]
    holder_match = held_here[None, :] & (slot_rank[None, :] == slot_ids)
    owner_read = jnp.sum(
        jnp.where(holder_match, (block_of * per_pair + pair_rank)[None, :], 0), axis=1
    )
    is_filled = jnp.any(holder_match, axis=1)
    return_match = (
        held_here[None, None, :]
        & (block_of[None, None, :] == dest_ids)
        & (pair_rank[None, None, :] == pair_ids)
    )
    owner_pick = jnp.sum(jnp.where(return_match, slot_rank[None, None, :], 0), axis=2).reshape(-1)
    return (local_pick, shard_read, owner_read, is_filled, owner_pick)


FIXED = 1.0 + OUTER_MOMENTUM
SQUARED = OUTER_MOMENTUM * OUTER_MOMENTUM


def flip(index, bits):
    out, unit = index, 1
    while unit <= bits:
        if bits & unit:
            out = out + unit - 2 * unit * ((index // unit) % 2)
        unit *= 2
    return out


def route_kernel(
    own_count, per_pair, groups,
    local_pick, shard_read, owner_read, filled, owner_pick, weights, anchor, momentum,
    emb_weights, emb_anchor, sketch, inv_root,
    new_weights, new_momentum, factor_out, basis_out,
    anchor_part, momentum_part, mine, core_in, chip_out, chip_in, mean, held_out, held_in,
    mean_out, gathered, fresh, anchor_all, momentum_all,
    local_sem, core_send, core_recv, chip_send, chip_recv, held_send, held_recv,
    mean_send, mean_recv, gc_send, gc_recv, gx_send, gx_recv, gf_send, gf_recv,
    fresh_send, fresh_recv, tile_sem, slot_sem,
    diff, sketch_own, sketch_half, sketch_core, sketch_chip, factor_own, factor_core,
    factor_half, factor_chip, factor_quarter, factor_in, factor_sum, factor_all,
    sk_send, sk_recv, fa_send, fa_recv, fr_send, fr_recv, fg_send, fg_recv, factor_sem,
):
    rep = lax.axis_index("rep")
    own = lax.axis_index("own")
    core_peer, chip_peer, far_peer = flip(rep, 1), flip(rep, 2), flip(rep, 3)
    tiles, part = mean.shape[0], mean.shape[2]
    slots = anchor_part.shape[0]

    def columns(index):
        return pl.ds(pl.multiple_of(index * part, 128), part)

    def to_rep(src, dst, send, recv, peer):
        return pltpu.make_async_remote_copy(
            src_ref=src, dst_ref=dst, send_sem=send, recv_sem=recv,
            device_id=(peer, own), device_id_type=pl.DeviceIdType.MESH,
        )

    def to_own(src, dst, send, recv, peer):
        return pltpu.make_async_remote_copy(
            src_ref=src, dst_ref=dst, send_sem=send, recv_sem=recv,
            device_id=(rep, peer), device_id_type=pl.DeviceIdType.MESH,
        )

    first = [
        pltpu.make_async_copy(anchor.at[:, :, columns(rep)], anchor_part, local_sem.at[0]),
        pltpu.make_async_copy(momentum.at[:, :, columns(rep)], momentum_part, local_sem.at[1]),
        pltpu.make_async_copy(weights.at[0, :, :, columns(rep)], mine.at[0], local_sem.at[2]),
        pltpu.make_async_copy(weights.at[0, :, :, columns(chip_peer)], mine.at[1], local_sem.at[3]),
    ]
    for copy in first:
        copy.start()

    barrier = pltpu.get_barrier_semaphore()
    for peer in (core_peer, chip_peer):
        pl.semaphore_signal(
            barrier, inc=1, device_id=(peer, own), device_id_type=pl.DeviceIdType.MESH
        )
    for k in range(1, own_count):
        pl.semaphore_signal(
            barrier, inc=1, device_id=(rep, flip(own, k)), device_id_type=pl.DeviceIdType.MESH
        )
    pl.semaphore_wait(barrier, own_count + 1)

    core_copies = [
        to_rep(
            weights.at[0, :, :, columns(source)], core_in.at[j], core_send.at[j],
            core_recv.at[j], core_peer,
        )
        for j, source in ((1, far_peer), (0, core_peer))
    ]
    for copy in core_copies:
        copy.start()

    highest = lax.Precision.HIGHEST
    f32 = jnp.float32
    diff[...] = emb_anchor[...] - emb_weights[0]
    sketched = jnp.zeros(sketch_own.shape, f32)
    for q in range(4):
        at = slice(q * part, (q + 1) * part)
        sketched = sketched + lax.dot_general(
            sketch[:, at], diff[:, at], (((1,), (1,)), ((), ())),
            precision=highest, preferred_element_type=f32,
        )
    sketch_own[...] = sketched
    small_copies = [to_rep(sketch_own, sketch_core, sk_send.at[0], sk_recv.at[0], core_peer)]
    small_copies[0].start()

    first[0].wait()
    first[1].wait()
    held_copies = []
    for k in list(range(1, own_count)) + [0]:
        peer = flip(own, k)

        def fill(p, carry, k=k, peer=peer):
            slot = owner_pick[peer * per_pair + p]
            a = anchor_part[slot]
            value = a - OUTER_RATE * (FIXED * a + SQUARED * momentum_part[slot])
            if k == 0:
                held_in[own * per_pair + p] = value
            else:
                held_out[k * per_pair + p] = value
            return carry

        lax.fori_loop(0, per_pair, fill, 0)
        if k:
            copy = to_own(
                held_out.at[pl.ds(k * per_pair, per_pair)],
                held_in.at[pl.ds(own * per_pair, per_pair)],
                held_send.at[k], held_recv.at[k], peer,
            )
            copy.start()
            held_copies.append(copy)

    whole = [
        pltpu.make_async_copy(anchor, anchor_all, local_sem.at[4]),
        pltpu.make_async_copy(momentum, momentum_all, local_sem.at[5]),
    ]
    for copy in whole:
        copy.start()

    small_copies[0].wait_recv()
    sketch_half[...] = sketch_own[...] + sketch_core[...]
    copy = to_rep(sketch_half, sketch_chip, sk_send.at[1], sk_recv.at[1], chip_peer)
    copy.start()
    small_copies.append(copy)

    first[2].wait()
    first[3].wait()
    core_copies[0].wait_recv()

    def half_sum(t, carry):
        chip_out[t] = mine[1, t] + core_in[1, t]
        return carry

    lax.fori_loop(0, tiles, half_sum, 0)
    chip_copy = to_rep(chip_out, chip_in, chip_send.at[0], chip_recv.at[0], chip_peer)
    chip_copy.start()

    small_copies[1].wait_recv()
    sketch_mean = (sketch_half[...] + sketch_chip[...]) * 0.25
    basis = jnp.dot(inv_root[...], sketch_mean, precision=highest, preferred_element_type=f32)
    basis_out[...] = basis
    chunks, chunk_rows = factor_own.shape[1:3]
    for q in range(4):
        value = jnp.dot(
            basis, diff[:, q * part : (q + 1) * part],
            precision=highest, preferred_element_type=f32,
        )
        for j in range(chunks):
            factor_own[q, j] = value[j * chunk_rows : (j + 1) * chunk_rows]
    for j, source in ((1, far_peer), (0, core_peer)):
        copy = to_rep(
            factor_own.at[source], factor_core.at[j], fa_send.at[j], fa_recv.at[j], core_peer
        )
        copy.start()
        small_copies.append(copy)
    small_copies[2].wait_recv()
    factor_half[...] = factor_own[chip_peer] + factor_core[1]
    copy = to_rep(factor_half, factor_chip, fa_send.at[2], fa_recv.at[2], chip_peer)
    copy.start()
    small_copies.append(copy)
    small_copies[3].wait_recv()

    core_copies[1].wait_recv()
    chip_copy.wait_recv()

    def full_sum(t, carry):
        mean[t] = (mine[0, t] + core_in[0, t] + chip_in[t]) * 0.25
        return carry

    lax.fori_loop(0, tiles, full_sum, 0)

    small_copies[4].wait_recv()
    factor_quarter[...] = factor_own[rep] + factor_core[0] + factor_chip[...]
    factor_in[own] = factor_quarter[own % chunks]
    part_copies = []
    for k in range(1, own_count):
        peer = flip(own, k)
        copy = to_own(
            factor_quarter.at[peer % chunks], factor_in.at[own], fr_send.at[k], fr_recv.at[k], peer
        )
        copy.start()
        part_copies.append(copy)

    mean_copies = {}
    for k in list(range(1, own_count)) + [0]:
        peer = flip(own, k)

        def fill_mean(p, carry, k=k, peer=peer):
            value = mean[local_pick[peer * per_pair + p]]
            if k == 0:
                gathered[rep, own * per_pair + p] = value
            else:
                mean_out[k * per_pair + p] = value
            return carry

        lax.fori_loop(0, per_pair, fill_mean, 0)
        if k:
            copy = to_own(
                mean_out.at[pl.ds(k * per_pair, per_pair)],
                gathered.at[rep, pl.ds(own * per_pair, per_pair)],
                mean_send.at[k], mean_recv.at[k], peer,
            )
            copy.start()
            mean_copies[k] = copy

    near, cross, passed = {}, {}, {}

    def spread(k):
        rows = pl.ds(flip(own, k) * per_pair, per_pair)
        if k:
            mean_copies[k].wait_recv()
        here = gathered.at[rep, rows]
        cross[k] = to_rep(here, here, gx_send.at[k], gx_recv.at[k], chip_peer)
        near[k] = to_rep(here, here, gc_send.at[k], gc_recv.at[k], core_peer)
        cross[k].start()
        near[k].start()

    def pass_on(k):
        rows = pl.ds(flip(own, k) * per_pair, per_pair)
        cross[k].wait_recv()
        there = gathered.at[chip_peer, rows]
        passed[k] = to_rep(there, there, gf_send.at[k], gf_recv.at[k], core_peer)
        passed[k].start()

    early = min(2, own_count)
    for k in range(early):
        spread(k)

    for copy in held_copies:
        copy.wait_recv()

    def renew(t, carry):
        fresh[rep, t] = held_in[shard_read[t]] + (OUTER_RATE * FIXED) * mean[t]
        return carry

    lax.fori_loop(0, tiles, renew, 0)
    fresh_copies = [
        to_rep(fresh.at[rep], fresh.at[rep], fresh_send.at[0], fresh_recv.at[0], chip_peer),
        to_rep(fresh.at[rep], fresh.at[rep], fresh_send.at[1], fresh_recv.at[1], core_peer),
    ]
    for copy in fresh_copies:
        copy.start()

    for copy in part_copies:
        copy.wait_recv()
    total = factor_in[0]
    for k in range(1, own_count):
        total = total + factor_in[k]
    factor_sum[...] = total * 0.25
    factor_all[rep, own % chunks] = total * 0.25
    group_copies = []
    for k in range(1, chunks):
        copy = to_own(
            factor_sum, factor_all.at[rep, own % chunks], fg_send.at[k], fg_recv.at[k], flip(own, k)
        )
        copy.start()
        group_copies.append(copy)

    for k in range(early, own_count):
        spread(k)
        pass_on(k - early)
    fresh_copies[0].wait_recv()
    last = to_rep(
        fresh.at[chip_peer], fresh.at[chip_peer], fresh_send.at[2], fresh_recv.at[2], core_peer
    )
    last.start()
    fresh_copies.append(last)
    for k in range(own_count - early, own_count):
        pass_on(k)

    for copy in group_copies:
        copy.wait_recv()
    for j, peer in ((3, chip_peer), (4, core_peer)):
        copy = to_rep(factor_all.at[rep], factor_all.at[rep], fa_send.at[j], fa_recv.at[j], peer)
        copy.start()
        small_copies.append(copy)

    fresh_copies[1].wait_recv()
    last.wait_recv()
    tile_copies = [
        pltpu.make_async_copy(
            fresh.at[q], new_weights.at[:, :, pl.ds(q * part, part)], tile_sem.at[q]
        )
        for q in range(4)
    ]
    for copy in tile_copies:
        copy.start()
    for copy in whole:
        copy.wait()
    for k in range(own_count):
        near[k].wait_recv()
        passed[k].wait_recv()

    small_copies[5].wait_recv()
    copy = to_rep(
        factor_all.at[chip_peer], factor_all.at[chip_peer], fa_send.at[5], fa_recv.at[5], core_peer
    )
    copy.start()
    small_copies.append(copy)

    size = slots // groups
    slot_copies = []
    for g in range(groups):

        def advance(j, carry, g=g):
            s = g * size + j
            row = owner_read[s]
            kept = jnp.full((8, 128), filled[s], jnp.int32) > 0
            kept = jnp.concatenate([kept.astype(jnp.float32)] * (part // 128), axis=1) > 0.5
            for q in range(4):
                at = pl.ds(q * part, part)
                moved = OUTER_MOMENTUM * momentum_all[s, :, at] + (
                    anchor_all[s, :, at] - gathered[q, row]
                )
                momentum_all[s, :, at] = jnp.where(kept, moved, 0.0)
            return carry

        lax.fori_loop(0, size, advance, 0)
        copy = pltpu.make_async_copy(
            momentum_all.at[pl.ds(g * size, size)],
            new_momentum.at[pl.ds(g * size, size)],
            slot_sem.at[g],
        )
        copy.start()
        slot_copies.append(copy)

    small_copies[6].wait_recv()
    small_copies[7].wait_recv()
    for q in range(4):
        copy = pltpu.make_async_copy(
            factor_all.at[q], factor_out.at[:, :, pl.ds(q * part, part)], factor_sem.at[q]
        )
        copy.start()
        tile_copies.append(copy)
    for copy in core_copies + [chip_copy] + held_copies + fresh_copies + small_copies:
        copy.wait_send()
    for copy in part_copies + group_copies:
        copy.wait_send()
    for k in range(own_count):
        if k:
            mean_copies[k].wait_send()
        near[k].wait_send()
        cross[k].wait_send()
        passed[k].wait_send()
    for copy in tile_copies + slot_copies:
        copy.wait()


def route(weights, anchor, momentum, embed, tables, own_count, per_pair):
    tiles, rows, width = weights.shape[1:]
    slots, part = anchor.shape[0], width // 4
    pairs = own_count * per_pair
    groups = 8 if slots % 8 == 0 else 1
    f32, dma = jnp.float32, pltpu.SemaphoreType.DMA
    scratch = [
        pltpu.VMEM((slots, rows, part), f32), pltpu.VMEM((slots, rows, part), f32),
        pltpu.VMEM((2, tiles, rows, part), f32), pltpu.VMEM((2, tiles, rows, part), f32),
        pltpu.VMEM((tiles, rows, part), f32), pltpu.VMEM((tiles, rows, part), f32),
        pltpu.VMEM((tiles, rows, part), f32),
        pltpu.VMEM((pairs, rows, part), f32), pltpu.VMEM((pairs, rows, part), f32),
        pltpu.VMEM((pairs, rows, part), f32), pltpu.VMEM((4, pairs, rows, part), f32),
        pltpu.VMEM((4, tiles, rows, part), f32),
        pltpu.VMEM((slots, rows, width), f32), pltpu.VMEM((slots, rows, width), f32),
        dma((6,)), dma((2,)), dma((2,)), dma((1,)), dma((1,)),
    ] + [dma((own_count,)) for _ in range(10)] + [dma((3,)), dma((3,)), dma((4,)), dma((groups,))]
    emb_rows, rank, chunks = embed[1].shape[0], embed[2].shape[0], 8
    chunk = (rank // chunks, part)
    scratch += [
        pltpu.VMEM((emb_rows, width), f32),
        pltpu.VMEM((rank, emb_rows), f32), pltpu.VMEM((rank, emb_rows), f32),
        pltpu.VMEM((rank, emb_rows), f32), pltpu.VMEM((rank, emb_rows), f32),
        pltpu.VMEM((4, chunks) + chunk, f32), pltpu.VMEM((2, chunks) + chunk, f32),
        pltpu.VMEM((chunks,) + chunk, f32), pltpu.VMEM((chunks,) + chunk, f32),
        pltpu.VMEM((chunks,) + chunk, f32), pltpu.VMEM((own_count,) + chunk, f32),
        pltpu.VMEM(chunk, f32), pltpu.VMEM((4, chunks) + chunk, f32),
        dma((2,)), dma((2,)), dma((6,)), dma((6,)), dma((own_count,)), dma((own_count,)),
        dma((chunks,)), dma((chunks,)), dma((4,)),
    ]
    return pl.pallas_call(
        functools.partial(route_kernel, own_count, per_pair, groups),
        out_shape=(
            jax.ShapeDtypeStruct((tiles, rows, width), f32),
            jax.ShapeDtypeStruct((slots, rows, width), f32),
            jax.ShapeDtypeStruct((chunks, rank // chunks, width), f32),
            jax.ShapeDtypeStruct((rank, emb_rows), f32),
        ),
        in_specs=[pl.BlockSpec(memory_space=pltpu.SMEM)] * 5 + [pl.BlockSpec(memory_space=pl.ANY)] * 3
        + [pl.BlockSpec(memory_space=pltpu.VMEM)] * 4,
        out_specs=(pl.BlockSpec(memory_space=pl.ANY),) * 3 + (pl.BlockSpec(memory_space=pltpu.VMEM),),
        scratch_shapes=scratch,
        compiler_params=pltpu.CompilerParams(
            collective_id=0, has_side_effects=True, vmem_limit_bytes=60 * 1024 * 1024
        ),
        cost_estimate=pl.CostEstimate(flops=20000000, bytes_accessed=300000000, transcendentals=0),
    )(*tables, weights, anchor, momentum, *embed)


def local(
    weights, anchor, momentum, owner, emb_weights, emb_anchor, emb_momentum, sketch, inv_root
):
    own_count = lax.axis_size("own")
    own_index = lax.axis_index("own")
    tiles_dev = weights.shape[1]
    capacity = anchor.shape[0]
    half_tiles = min(tiles_dev // 2, own_count)
    hot_count = max(own_count // 4, 1)
    per_pair = (tiles_dev - half_tiles) // hot_count + 1
    local_pick, shard_read, owner_read, is_filled, owner_pick = owner_tables(
        owner, tiles_dev, per_pair, capacity, own_index, own_count
    )
    tables = (local_pick, shard_read, owner_read, is_filled.astype(jnp.int32), owner_pick)
    embed = (emb_weights, emb_anchor, sketch, inv_root)
    new_weights, new_momentum, factor, basis_rows = route(
        weights, anchor, momentum, embed, tables, own_count, per_pair
    )
    factor = factor.reshape(sketch.shape)
    highest = lax.Precision.HIGHEST
    approx = lax.dot_general(
        basis_rows,
        factor,
        (((0,), (0,)), ((), ())),
        precision=highest,
        preferred_element_type=jnp.float32,
    )
    new_emb_momentum = OUTER_MOMENTUM * emb_momentum + approx
    new_embedding = emb_anchor - OUTER_RATE * (approx + OUTER_MOMENTUM * new_emb_momentum)
    return (new_weights, new_momentum, new_embedding, new_emb_momentum)


def solution(mesh):
    placed = (
        P("rep", "own", None, None),
        P("own", None, None),
        P("own", None, None),
        P(),
        P("rep", "own", None),
        P("own", None),
        P("own", None),
        P(),
        P(),
    )
    return jax.shard_map(
        local,
        mesh=mesh,
        in_specs=placed,
        out_specs=(P("own", None, None), P("own", None, None), P("own", None), P("own", None)),
        check_vma=False,
    )
```

```python
import functools

import jax
import jax.numpy as jnp
from jax import lax
from jax.experimental import pallas as pl
from jax.experimental.pallas import tpu as pltpu
from jax.sharding import PartitionSpec as P

OUTER_RATE = 0.7
OUTER_MOMENTUM = 0.9


def owner_tables(owner, tiles_dev, per_pair, capacity, own_index, own_count):
    tile_count = owner.shape[0]
    tile_ids = jnp.arange(tile_count, dtype=jnp.int32)
    block_of = tile_ids // tiles_dev
    same_owner = owner[:, None] == owner[None, :]
    earlier = tile_ids[None, :] < tile_ids[:, None]
    slot_rank = jnp.sum(same_owner & earlier, axis=1, dtype=jnp.int32)
    pair_rank = jnp.sum(
        same_owner & earlier & (block_of[:, None] == block_of[None, :]), axis=1, dtype=jnp.int32
    )
    pair_key = owner * per_pair + pair_rank
    back_key = block_of * per_pair + pair_rank
    held_here = owner == own_index
    local_key = jnp.where(block_of == own_index, pair_key, -1)
    held_key = jnp.where(held_here, back_key, -1)
    slot_key = jnp.where(held_here, slot_rank, -1)
    pair_ids = jnp.arange(own_count * per_pair, dtype=jnp.int32)[:, None]
    slot_ids = jnp.arange(capacity, dtype=jnp.int32)[:, None]

    def look_up(ids, key, value):
        return jnp.sum(jnp.where(key[None, :] == ids, value[None, :], 0), axis=1, dtype=jnp.int32)

    local_pick = look_up(pair_ids, local_key, tile_ids - own_index * tiles_dev)
    owner_pick = look_up(pair_ids, held_key, slot_rank)
    owner_read = look_up(slot_ids, slot_key, back_key + 1)
    return (local_pick, pair_key, owner_read, owner_pick)


FIXED = 1.0 + OUTER_MOMENTUM
SQUARED = OUTER_MOMENTUM * OUTER_MOMENTUM


def flip(index, bits):
    out, unit = index, 1
    while unit <= bits:
        if bits & unit:
            out = out + unit - 2 * unit * ((index // unit) % 2)
        unit *= 2
    return out


def route_kernel(
    own_count, per_pair, groups,
    local_pick, pair_key, owner_read, owner_pick, weights, anchor, momentum,
    emb_weights, emb_anchor, sketch, inv_root,
    new_weights, new_momentum, factor_out, basis_out,
    anchor_part, momentum_part, mine, core_in, chip_out, chip_in, mean, held_out, held_in,
    mean_out, gathered, fresh, anchor_all, momentum_all,
    local_sem, core_send, core_recv, chip_send, chip_recv, held_send, held_recv,
    mean_send, mean_recv, gc_send, gc_recv, gx_send, gx_recv, gf_send, gf_recv,
    fresh_send, fresh_recv, tile_sem, slot_sem,
    diff, sketch_own, sketch_half, sketch_core, sketch_chip, factor_own, factor_core,
    factor_half, factor_chip, factor_quarter, factor_in, factor_sum, factor_all,
    sk_send, sk_recv, fa_send, fa_recv, fr_send, fr_recv, fg_send, fg_recv, factor_sem,
):
    rep = lax.axis_index("rep")
    own = lax.axis_index("own")
    core_peer, chip_peer, far_peer = flip(rep, 1), flip(rep, 2), flip(rep, 3)
    tiles, part = mean.shape[0], mean.shape[2]
    slots = anchor_part.shape[0]

    def columns(index):
        return pl.ds(pl.multiple_of(index * part, 128), part)

    def to_rep(src, dst, send, recv, peer):
        return pltpu.make_async_remote_copy(
            src_ref=src, dst_ref=dst, send_sem=send, recv_sem=recv,
            device_id=(peer, own), device_id_type=pl.DeviceIdType.MESH,
        )

    def to_own(src, dst, send, recv, peer):
        return pltpu.make_async_remote_copy(
            src_ref=src, dst_ref=dst, send_sem=send, recv_sem=recv,
            device_id=(rep, peer), device_id_type=pl.DeviceIdType.MESH,
        )

    first = [
        pltpu.make_async_copy(anchor.at[:, :, columns(rep)], anchor_part, local_sem.at[0]),
        pltpu.make_async_copy(momentum.at[:, :, columns(rep)], momentum_part, local_sem.at[1]),
        pltpu.make_async_copy(weights.at[0, :, :, columns(rep)], mine.at[0], local_sem.at[2]),
        pltpu.make_async_copy(weights.at[0, :, :, columns(chip_peer)], mine.at[1], local_sem.at[3]),
    ]
    for copy in first:
        copy.start()

    barrier = pltpu.get_barrier_semaphore()
    for peer in (core_peer, chip_peer):
        pl.semaphore_signal(
            barrier, inc=1, device_id=(peer, own), device_id_type=pl.DeviceIdType.MESH
        )
    for k in range(1, own_count):
        pl.semaphore_signal(
            barrier, inc=1, device_id=(rep, flip(own, k)), device_id_type=pl.DeviceIdType.MESH
        )
    pl.semaphore_wait(barrier, own_count + 1)

    core_copies = [
        to_rep(
            weights.at[0, :, :, columns(source)], core_in.at[j], core_send.at[j],
            core_recv.at[j], core_peer,
        )
        for j, source in ((1, far_peer), (0, core_peer))
    ]
    for copy in core_copies:
        copy.start()

    first[0].wait()
    first[1].wait()
    held_copies = []
    for k in list(range(1, own_count)) + [0]:
        peer = flip(own, k)

        def fill(p, carry, k=k, peer=peer):
            slot = owner_pick[peer * per_pair + p]
            a = anchor_part[slot]
            value = a - OUTER_RATE * (FIXED * a + SQUARED * momentum_part[slot])
            if k == 0:
                held_in[own * per_pair + p] = value
            else:
                held_out[k * per_pair + p] = value
            return carry

        lax.fori_loop(0, per_pair, fill, 0)
        if k:
            copy = to_own(
                held_out.at[pl.ds(k * per_pair, per_pair)],
                held_in.at[pl.ds(own * per_pair, per_pair)],
                held_send.at[k], held_recv.at[k], peer,
            )
            copy.start()
            held_copies.append(copy)

    highest = lax.Precision.HIGHEST
    f32 = jnp.float32
    diff[...] = emb_anchor[...] - emb_weights[0]
    sketched = jnp.zeros(sketch_own.shape, f32)
    for q in range(4):
        at = slice(q * part, (q + 1) * part)
        sketched = sketched + lax.dot_general(
            sketch[:, at], diff[:, at], (((1,), (1,)), ((), ())),
            precision=highest, preferred_element_type=f32,
        )
    sketch_own[...] = sketched
    small_copies = [to_rep(sketch_own, sketch_core, sk_send.at[0], sk_recv.at[0], core_peer)]
    small_copies[0].start()

    whole = [
        pltpu.make_async_copy(anchor, anchor_all, local_sem.at[4]),
        pltpu.make_async_copy(momentum, momentum_all, local_sem.at[5]),
    ]
    for copy in whole:
        copy.start()

    small_copies[0].wait_recv()
    sketch_half[...] = sketch_own[...] + sketch_core[...]
    copy = to_rep(sketch_half, sketch_chip, sk_send.at[1], sk_recv.at[1], chip_peer)
    copy.start()
    small_copies.append(copy)

    first[2].wait()
    first[3].wait()
    core_copies[0].wait_recv()

    def half_sum(t, carry):
        chip_out[t] = mine[1, t] + core_in[1, t]
        return carry

    lax.fori_loop(0, tiles, half_sum, 0)
    chip_copy = to_rep(chip_out, chip_in, chip_send.at[0], chip_recv.at[0], chip_peer)
    chip_copy.start()

    small_copies[1].wait_recv()
    sketch_mean = (sketch_half[...] + sketch_chip[...]) * 0.25
    basis = jnp.dot(inv_root[...], sketch_mean, precision=highest, preferred_element_type=f32)
    basis_out[...] = basis
    chunks, chunk_rows = factor_own.shape[1:3]
    for q in range(4):
        value = jnp.dot(
            basis, diff[:, q * part : (q + 1) * part],
            precision=highest, preferred_element_type=f32,
        )
        for j in range(chunks):
            factor_own[q, j] = value[j * chunk_rows : (j + 1) * chunk_rows]
    for j, source in ((1, far_peer), (0, core_peer)):
        copy = to_rep(
            factor_own.at[source], factor_core.at[j], fa_send.at[j], fa_recv.at[j], core_peer
        )
        copy.start()
        small_copies.append(copy)
    small_copies[2].wait_recv()
    factor_half[...] = factor_own[chip_peer] + factor_core[1]
    copy = to_rep(factor_half, factor_chip, fa_send.at[2], fa_recv.at[2], chip_peer)
    copy.start()
    small_copies.append(copy)
    small_copies[3].wait_recv()

    core_copies[1].wait_recv()
    chip_copy.wait_recv()

    def full_sum(t, carry):
        mean[t] = (mine[0, t] + core_in[0, t] + chip_in[t]) * 0.25
        return carry

    lax.fori_loop(0, tiles, full_sum, 0)

    small_copies[4].wait_recv()
    factor_quarter[...] = factor_own[rep] + factor_core[0] + factor_chip[...]
    factor_in[own] = factor_quarter[own % chunks]
    part_copies = []
    for k in range(1, own_count):
        peer = flip(own, k)
        copy = to_own(
            factor_quarter.at[peer % chunks], factor_in.at[own], fr_send.at[k], fr_recv.at[k], peer
        )
        copy.start()
        part_copies.append(copy)

    mean_copies = {}
    for k in list(range(1, own_count)) + [0]:
        peer = flip(own, k)

        def fill_mean(p, carry, k=k, peer=peer):
            value = mean[local_pick[peer * per_pair + p]]
            if k == 0:
                gathered[rep, own * per_pair + p] = value
            else:
                mean_out[k * per_pair + p] = value
            return carry

        lax.fori_loop(0, per_pair, fill_mean, 0)
        if k:
            copy = to_own(
                mean_out.at[pl.ds(k * per_pair, per_pair)],
                gathered.at[rep, pl.ds(own * per_pair, per_pair)],
                mean_send.at[k], mean_recv.at[k], peer,
            )
            copy.start()
            mean_copies[k] = copy

    near, cross, passed = {}, {}, {}

    def spread(k):
        rows = pl.ds(flip(own, k) * per_pair, per_pair)
        if k:
            mean_copies[k].wait_recv()
        here = gathered.at[rep, rows]
        cross[k] = to_rep(here, here, gx_send.at[k], gx_recv.at[k], chip_peer)
        near[k] = to_rep(here, here, gc_send.at[k], gc_recv.at[k], core_peer)
        cross[k].start()
        near[k].start()

    def pass_on(k):
        rows = pl.ds(flip(own, k) * per_pair, per_pair)
        cross[k].wait_recv()
        there = gathered.at[chip_peer, rows]
        passed[k] = to_rep(there, there, gf_send.at[k], gf_recv.at[k], core_peer)
        passed[k].start()

    early = min(2, own_count)
    for k in range(early):
        spread(k)

    for copy in held_copies:
        copy.wait_recv()

    def renew(t, carry):
        fresh[rep, t] = held_in[pair_key[own * tiles + t]] + (OUTER_RATE * FIXED) * mean[t]
        return carry

    lax.fori_loop(0, tiles, renew, 0)
    fresh_copies = [
        to_rep(fresh.at[rep], fresh.at[rep], fresh_send.at[0], fresh_recv.at[0], chip_peer),
        to_rep(fresh.at[rep], fresh.at[rep], fresh_send.at[1], fresh_recv.at[1], core_peer),
    ]
    for copy in fresh_copies:
        copy.start()

    for copy in part_copies:
        copy.wait_recv()
    total = factor_in[0]
    for k in range(1, own_count):
        total = total + factor_in[k]
    factor_sum[...] = total * 0.25
    factor_all[rep, own % chunks] = total * 0.25
    group_copies = []
    for k in range(1, chunks):
        copy = to_own(
            factor_sum, factor_all.at[rep, own % chunks], fg_send.at[k], fg_recv.at[k], flip(own, k)
        )
        copy.start()
        group_copies.append(copy)

    for k in range(early, own_count):
        spread(k)
        pass_on(k - early)
    fresh_copies[0].wait_recv()
    last = to_rep(
        fresh.at[chip_peer], fresh.at[chip_peer], fresh_send.at[2], fresh_recv.at[2], core_peer
    )
    last.start()
    fresh_copies.append(last)
    for k in range(own_count - early, own_count):
        pass_on(k)

    for copy in group_copies:
        copy.wait_recv()
    for j, peer in ((3, chip_peer), (4, core_peer)):
        copy = to_rep(factor_all.at[rep], factor_all.at[rep], fa_send.at[j], fa_recv.at[j], peer)
        copy.start()
        small_copies.append(copy)

    fresh_copies[1].wait_recv()
    last.wait_recv()
    tile_copies = [
        pltpu.make_async_copy(
            fresh.at[q], new_weights.at[:, :, pl.ds(q * part, part)], tile_sem.at[q]
        )
        for q in range(4)
    ]
    for copy in tile_copies:
        copy.start()
    for copy in whole:
        copy.wait()
    for k in range(own_count):
        near[k].wait_recv()
        passed[k].wait_recv()

    small_copies[5].wait_recv()
    copy = to_rep(
        factor_all.at[chip_peer], factor_all.at[chip_peer], fa_send.at[5], fa_recv.at[5], core_peer
    )
    copy.start()
    small_copies.append(copy)

    size = slots // groups
    slot_copies = []
    for g in range(groups):

        def advance(j, carry, g=g):
            s = g * size + j
            found = owner_read[s]
            row = jnp.maximum(found - 1, 0)
            kept = jnp.full((momentum_all.shape[1], part), found, jnp.int32) > 0
            for q in range(4):
                at = pl.ds(q * part, part)
                moved = OUTER_MOMENTUM * momentum_all[s, :, at] + (
                    anchor_all[s, :, at] - gathered[q, row]
                )
                momentum_all[s, :, at] = jnp.where(kept, moved, 0.0)
            return carry

        lax.fori_loop(0, size, advance, 0)
        copy = pltpu.make_async_copy(
            momentum_all.at[pl.ds(g * size, size)],
            new_momentum.at[pl.ds(g * size, size)],
            slot_sem.at[g],
        )
        copy.start()
        slot_copies.append(copy)

    small_copies[6].wait_recv()
    small_copies[7].wait_recv()
    for q in range(4):
        copy = pltpu.make_async_copy(
            factor_all.at[q], factor_out.at[:, :, pl.ds(q * part, part)], factor_sem.at[q]
        )
        copy.start()
        tile_copies.append(copy)
    for copy in core_copies + [chip_copy] + held_copies + fresh_copies + small_copies:
        copy.wait_send()
    for copy in part_copies + group_copies:
        copy.wait_send()
    for k in range(own_count):
        if k:
            mean_copies[k].wait_send()
        near[k].wait_send()
        cross[k].wait_send()
        passed[k].wait_send()
    for copy in tile_copies + slot_copies:
        copy.wait()


def route(weights, anchor, momentum, embed, tables, own_count, per_pair):
    tiles, rows, width = weights.shape[1:]
    slots, part = anchor.shape[0], width // 4
    pairs = own_count * per_pair
    groups = 8 if slots % 8 == 0 else 1
    f32, dma = jnp.float32, pltpu.SemaphoreType.DMA
    scratch = [
        pltpu.VMEM((slots, rows, part), f32), pltpu.VMEM((slots, rows, part), f32),
        pltpu.VMEM((2, tiles, rows, part), f32), pltpu.VMEM((2, tiles, rows, part), f32),
        pltpu.VMEM((tiles, rows, part), f32), pltpu.VMEM((tiles, rows, part), f32),
        pltpu.VMEM((tiles, rows, part), f32),
        pltpu.VMEM((pairs, rows, part), f32), pltpu.VMEM((pairs, rows, part), f32),
        pltpu.VMEM((pairs, rows, part), f32), pltpu.VMEM((4, pairs, rows, part), f32),
        pltpu.VMEM((4, tiles, rows, part), f32),
        pltpu.VMEM((slots, rows, width), f32), pltpu.VMEM((slots, rows, width), f32),
        dma((6,)), dma((2,)), dma((2,)), dma((1,)), dma((1,)),
    ] + [dma((own_count,)) for _ in range(10)] + [dma((3,)), dma((3,)), dma((4,)), dma((groups,))]
    emb_rows, rank, chunks = embed[1].shape[0], embed[2].shape[0], 8
    chunk = (rank // chunks, part)
    scratch += [
        pltpu.VMEM((emb_rows, width), f32),
        pltpu.VMEM((rank, emb_rows), f32), pltpu.VMEM((rank, emb_rows), f32),
        pltpu.VMEM((rank, emb_rows), f32), pltpu.VMEM((rank, emb_rows), f32),
        pltpu.VMEM((4, chunks) + chunk, f32), pltpu.VMEM((2, chunks) + chunk, f32),
        pltpu.VMEM((chunks,) + chunk, f32), pltpu.VMEM((chunks,) + chunk, f32),
        pltpu.VMEM((chunks,) + chunk, f32), pltpu.VMEM((own_count,) + chunk, f32),
        pltpu.VMEM(chunk, f32), pltpu.VMEM((4, chunks) + chunk, f32),
        dma((2,)), dma((2,)), dma((6,)), dma((6,)), dma((own_count,)), dma((own_count,)),
        dma((chunks,)), dma((chunks,)), dma((4,)),
    ]
    return pl.pallas_call(
        functools.partial(route_kernel, own_count, per_pair, groups),
        out_shape=(
            jax.ShapeDtypeStruct((tiles, rows, width), f32),
            jax.ShapeDtypeStruct((slots, rows, width), f32),
            jax.ShapeDtypeStruct((chunks, rank // chunks, width), f32),
            jax.ShapeDtypeStruct((rank, emb_rows), f32),
        ),
        in_specs=[pl.BlockSpec(memory_space=pltpu.SMEM)] * 4 + [pl.BlockSpec(memory_space=pl.ANY)] * 3
        + [pl.BlockSpec(memory_space=pltpu.VMEM)] * 4,
        out_specs=(pl.BlockSpec(memory_space=pl.ANY),) * 3 + (pl.BlockSpec(memory_space=pltpu.VMEM),),
        scratch_shapes=scratch,
        compiler_params=pltpu.CompilerParams(
            collective_id=0, has_side_effects=True, vmem_limit_bytes=60 * 1024 * 1024
        ),
        cost_estimate=pl.CostEstimate(flops=20000000, bytes_accessed=300000000, transcendentals=0),
    )(*tables, weights, anchor, momentum, *embed)


def local(
    weights, anchor, momentum, owner, emb_weights, emb_anchor, emb_momentum, sketch, inv_root
):
    own_count = lax.axis_size("own")
    own_index = lax.axis_index("own")
    tiles_dev = weights.shape[1]
    capacity = anchor.shape[0]
    half_tiles = min(tiles_dev // 2, own_count)
    hot_count = max(own_count // 4, 1)
    per_pair = (tiles_dev - half_tiles) // hot_count + 1
    tables = owner_tables(owner, tiles_dev, per_pair, capacity, own_index, own_count)
    embed = (emb_weights, emb_anchor, sketch, inv_root)
    new_weights, new_momentum, factor, basis_rows = route(
        weights, anchor, momentum, embed, tables, own_count, per_pair
    )
    factor = factor.reshape(sketch.shape)
    highest = lax.Precision.HIGHEST
    approx = lax.dot_general(
        basis_rows,
        factor,
        (((0,), (0,)), ((), ())),
        precision=highest,
        preferred_element_type=jnp.float32,
    )
    new_emb_momentum = OUTER_MOMENTUM * emb_momentum + approx
    new_embedding = emb_anchor - OUTER_RATE * (approx + OUTER_MOMENTUM * new_emb_momentum)
    return (new_weights, new_momentum, new_embedding, new_emb_momentum)


def solution(mesh):
    placed = (
        P("rep", "own", None, None),
        P("own", None, None),
        P("own", None, None),
        P(),
        P("rep", "own", None),
        P("own", None),
        P("own", None),
        P(),
        P(),
    )
    return jax.shard_map(
        local,
        mesh=mesh,
        in_specs=placed,
        out_specs=(P("own", None, None), P("own", None, None), P("own", None), P("own", None)),
        check_vma=False,
    )
```

```python
import functools

import jax
import jax.numpy as jnp
from jax import lax
from jax.experimental import pallas as pl
from jax.experimental.pallas import tpu as pltpu
from jax.sharding import PartitionSpec as P

OUTER_RATE = 0.7
OUTER_MOMENTUM = 0.9


def owner_tables(owner, tiles_dev, per_pair, capacity, own_index, own_count):
    tile_count = owner.shape[0]
    tile_ids = jnp.arange(tile_count, dtype=jnp.int32)
    block_of = tile_ids // tiles_dev
    same_owner = owner[:, None] == owner[None, :]
    earlier = tile_ids[None, :] < tile_ids[:, None]
    slot_rank = jnp.sum(same_owner & earlier, axis=1, dtype=jnp.int32)
    pair_rank = jnp.sum(
        same_owner & earlier & (block_of[:, None] == block_of[None, :]), axis=1, dtype=jnp.int32
    )
    pair_key = owner * per_pair + pair_rank
    back_key = block_of * per_pair + pair_rank
    held_here = owner == own_index
    local_key = jnp.where(block_of == own_index, pair_key, -1)
    held_key = jnp.where(held_here, back_key, -1)
    slot_key = jnp.where(held_here, slot_rank, -1)
    pair_ids = jnp.arange(own_count * per_pair, dtype=jnp.int32)[:, None]
    slot_ids = jnp.arange(capacity, dtype=jnp.int32)[:, None]

    def look_up(ids, key, value):
        return jnp.sum(jnp.where(key[None, :] == ids, value[None, :], 0), axis=1, dtype=jnp.int32)

    local_pick = look_up(pair_ids, local_key, tile_ids - own_index * tiles_dev)
    owner_pick = look_up(pair_ids, held_key, slot_rank)
    owner_read = look_up(slot_ids, slot_key, back_key + 1)
    return (local_pick, pair_key, owner_read, owner_pick)


FIXED = 1.0 + OUTER_MOMENTUM
SQUARED = OUTER_MOMENTUM * OUTER_MOMENTUM


def flip(index, bits):
    out, unit = index, 1
    while unit <= bits:
        if bits & unit:
            out = out + unit - 2 * unit * ((index // unit) % 2)
        unit *= 2
    return out


def route_kernel(
    own_count, per_pair, groups,
    local_pick, pair_key, owner_read, owner_pick, weights, anchor, momentum,
    emb_weights, emb_anchor, sketch, inv_root,
    new_weights, new_momentum, factor_out, basis_out,
    anchor_part, momentum_part, mine, core_in, chip_out, chip_in, mean, held_out, held_in,
    mean_out, gathered, fresh, anchor_all, momentum_all,
    local_sem, core_send, core_recv, chip_send, chip_recv, held_send, held_recv,
    mean_send, mean_recv, gc_send, gc_recv, gx_send, gx_recv, gf_send, gf_recv,
    fresh_send, fresh_recv, tile_sem, slot_sem,
    diff, sketch_own, sketch_half, sketch_core, sketch_chip, factor_own, factor_core,
    factor_half, factor_chip, factor_quarter, factor_in, factor_sum, factor_all,
    sk_send, sk_recv, fa_send, fa_recv, fr_send, fr_recv, fg_send, fg_recv, factor_sem,
):
    rep = lax.axis_index("rep")
    own = lax.axis_index("own")
    core_peer, chip_peer, far_peer = flip(rep, 1), flip(rep, 2), flip(rep, 3)
    tiles, part = mean.shape[0], mean.shape[2]
    slots = anchor_part.shape[0]

    def columns(index):
        return pl.ds(pl.multiple_of(index * part, 128), part)

    def to_rep(src, dst, send, recv, peer):
        return pltpu.make_async_remote_copy(
            src_ref=src, dst_ref=dst, send_sem=send, recv_sem=recv,
            device_id=(peer, own), device_id_type=pl.DeviceIdType.MESH,
        )

    def to_own(src, dst, send, recv, peer):
        return pltpu.make_async_remote_copy(
            src_ref=src, dst_ref=dst, send_sem=send, recv_sem=recv,
            device_id=(rep, peer), device_id_type=pl.DeviceIdType.MESH,
        )

    first = [
        pltpu.make_async_copy(anchor.at[:, :, columns(rep)], anchor_part, local_sem.at[0]),
        pltpu.make_async_copy(momentum.at[:, :, columns(rep)], momentum_part, local_sem.at[1]),
        pltpu.make_async_copy(weights.at[0, :, :, columns(rep)], mine.at[0], local_sem.at[2]),
        pltpu.make_async_copy(weights.at[0, :, :, columns(chip_peer)], mine.at[1], local_sem.at[3]),
    ]
    for copy in first:
        copy.start()

    barrier = pltpu.get_barrier_semaphore()
    for peer in (core_peer, chip_peer):
        pl.semaphore_signal(
            barrier, inc=1, device_id=(peer, own), device_id_type=pl.DeviceIdType.MESH
        )
    for k in range(1, own_count):
        pl.semaphore_signal(
            barrier, inc=1, device_id=(rep, flip(own, k)), device_id_type=pl.DeviceIdType.MESH
        )
    pl.semaphore_wait(barrier, own_count + 1)

    core_copies = [
        to_rep(
            weights.at[0, :, :, columns(source)], core_in.at[j], core_send.at[j],
            core_recv.at[j], core_peer,
        )
        for j, source in ((1, far_peer), (0, core_peer))
    ]
    for copy in core_copies:
        copy.start()

    first[0].wait()
    first[1].wait()
    held_copies = []
    for k in list(range(1, own_count)) + [0]:
        peer = flip(own, k)

        def fill(p, carry, k=k, peer=peer):
            slot = owner_pick[peer * per_pair + p]
            a = anchor_part[slot]
            value = a - OUTER_RATE * (FIXED * a + SQUARED * momentum_part[slot])
            if k == 0:
                held_in[own * per_pair + p] = value
            else:
                held_out[k * per_pair + p] = value
            return carry

        lax.fori_loop(0, per_pair, fill, 0)
        if k:
            copy = to_own(
                held_out.at[pl.ds(k * per_pair, per_pair)],
                held_in.at[pl.ds(own * per_pair, per_pair)],
                held_send.at[k], held_recv.at[k], peer,
            )
            copy.start()
            held_copies.append(copy)

    highest = lax.Precision.HIGHEST
    f32 = jnp.float32
    diff[...] = emb_anchor[...] - emb_weights[0]
    sketched = jnp.zeros(sketch_own.shape, f32)
    for q in range(4):
        at = slice(q * part, (q + 1) * part)
        sketched = sketched + lax.dot_general(
            sketch[:, at], diff[:, at], (((1,), (1,)), ((), ())),
            precision=highest, preferred_element_type=f32,
        )
    sketch_own[...] = sketched
    small_copies = [to_rep(sketch_own, sketch_core, sk_send.at[0], sk_recv.at[0], core_peer)]
    small_copies[0].start()

    whole = [
        pltpu.make_async_copy(anchor, anchor_all, local_sem.at[4]),
        pltpu.make_async_copy(momentum, momentum_all, local_sem.at[5]),
    ]
    for copy in whole:
        copy.start()

    small_copies[0].wait_recv()
    sketch_half[...] = sketch_own[...] + sketch_core[...]
    copy = to_rep(sketch_half, sketch_chip, sk_send.at[1], sk_recv.at[1], chip_peer)
    copy.start()
    small_copies.append(copy)

    first[2].wait()
    first[3].wait()
    core_copies[0].wait_recv()

    def half_sum(t, carry):
        chip_out[t] = mine[1, t] + core_in[1, t]
        return carry

    lax.fori_loop(0, tiles, half_sum, 0)
    chip_copy = to_rep(chip_out, chip_in, chip_send.at[0], chip_recv.at[0], chip_peer)
    chip_copy.start()

    small_copies[1].wait_recv()
    sketch_mean = (sketch_half[...] + sketch_chip[...]) * 0.25
    basis = jnp.dot(inv_root[...], sketch_mean, precision=highest, preferred_element_type=f32)
    basis_out[...] = basis
    chunks, chunk_rows = factor_own.shape[1:3]
    for q in range(4):
        value = jnp.dot(
            basis, diff[:, q * part : (q + 1) * part],
            precision=highest, preferred_element_type=f32,
        )
        for j in range(chunks):
            factor_own[q, j] = value[j * chunk_rows : (j + 1) * chunk_rows]
    for j, source in ((1, far_peer), (0, core_peer)):
        copy = to_rep(
            factor_own.at[source], factor_core.at[j], fa_send.at[j], fa_recv.at[j], core_peer
        )
        copy.start()
        small_copies.append(copy)
    small_copies[2].wait_recv()
    factor_half[...] = factor_own[chip_peer] + factor_core[1]
    copy = to_rep(factor_half, factor_chip, fa_send.at[2], fa_recv.at[2], chip_peer)
    copy.start()
    small_copies.append(copy)
    small_copies[3].wait_recv()

    core_copies[1].wait_recv()
    chip_copy.wait_recv()

    def full_sum(t, carry):
        mean[t] = (mine[0, t] + core_in[0, t] + chip_in[t]) * 0.25
        return carry

    lax.fori_loop(0, tiles, full_sum, 0)

    small_copies[4].wait_recv()
    factor_quarter[...] = factor_own[rep] + factor_core[0] + factor_chip[...]
    factor_in[own] = factor_quarter[own % chunks]
    part_copies = []
    for k in range(1, own_count):
        peer = flip(own, k)
        copy = to_own(
            factor_quarter.at[peer % chunks], factor_in.at[own], fr_send.at[k], fr_recv.at[k], peer
        )
        copy.start()
        part_copies.append(copy)

    mean_copies = {}
    for k in list(range(1, own_count)) + [0]:
        peer = flip(own, k)

        def fill_mean(p, carry, k=k, peer=peer):
            value = mean[local_pick[peer * per_pair + p]]
            if k == 0:
                gathered[rep, own * per_pair + p] = value
            else:
                mean_out[k * per_pair + p] = value
            return carry

        lax.fori_loop(0, per_pair, fill_mean, 0)
        if k:
            copy = to_own(
                mean_out.at[pl.ds(k * per_pair, per_pair)],
                gathered.at[rep, pl.ds(own * per_pair, per_pair)],
                mean_send.at[k], mean_recv.at[k], peer,
            )
            copy.start()
            mean_copies[k] = copy

    near, cross, passed = {}, {}, {}

    def spread(k):
        rows = pl.ds(flip(own, k) * per_pair, per_pair)
        if k:
            mean_copies[k].wait_recv()
        here = gathered.at[rep, rows]
        cross[k] = to_rep(here, here, gx_send.at[k], gx_recv.at[k], chip_peer)
        near[k] = to_rep(here, here, gc_send.at[k], gc_recv.at[k], core_peer)
        cross[k].start()
        near[k].start()

    def pass_on(k):
        rows = pl.ds(flip(own, k) * per_pair, per_pair)
        cross[k].wait_recv()
        there = gathered.at[chip_peer, rows]
        passed[k] = to_rep(there, there, gf_send.at[k], gf_recv.at[k], core_peer)
        passed[k].start()

    early = min(4, own_count)
    for k in range(early):
        spread(k)

    for copy in held_copies:
        copy.wait_recv()

    def renew(t, carry):
        fresh[rep, t] = held_in[pair_key[own * tiles + t]] + (OUTER_RATE * FIXED) * mean[t]
        return carry

    lax.fori_loop(0, tiles, renew, 0)
    fresh_copies = [
        to_rep(fresh.at[rep], fresh.at[rep], fresh_send.at[0], fresh_recv.at[0], chip_peer),
        to_rep(fresh.at[rep], fresh.at[rep], fresh_send.at[1], fresh_recv.at[1], core_peer),
    ]
    for copy in fresh_copies:
        copy.start()

    for copy in part_copies:
        copy.wait_recv()
    total = factor_in[0]
    for k in range(1, own_count):
        total = total + factor_in[k]
    factor_sum[...] = total * 0.25
    factor_all[rep, own % chunks] = total * 0.25
    group_copies = []
    for k in range(1, chunks):
        copy = to_own(
            factor_sum, factor_all.at[rep, own % chunks], fg_send.at[k], fg_recv.at[k], flip(own, k)
        )
        copy.start()
        group_copies.append(copy)

    for k in range(early, own_count):
        spread(k)
        pass_on(k - early)
    fresh_copies[0].wait_recv()
    last = to_rep(
        fresh.at[chip_peer], fresh.at[chip_peer], fresh_send.at[2], fresh_recv.at[2], core_peer
    )
    last.start()
    fresh_copies.append(last)
    for k in range(own_count - early, own_count):
        pass_on(k)

    for copy in group_copies:
        copy.wait_recv()
    for j, peer in ((3, chip_peer), (4, core_peer)):
        copy = to_rep(factor_all.at[rep], factor_all.at[rep], fa_send.at[j], fa_recv.at[j], peer)
        copy.start()
        small_copies.append(copy)

    fresh_copies[1].wait_recv()
    last.wait_recv()
    tile_copies = [
        pltpu.make_async_copy(
            fresh.at[q], new_weights.at[:, :, pl.ds(q * part, part)], tile_sem.at[q]
        )
        for q in range(4)
    ]
    for copy in tile_copies:
        copy.start()
    for copy in whole:
        copy.wait()
    for k in range(own_count):
        near[k].wait_recv()
        passed[k].wait_recv()

    small_copies[5].wait_recv()
    copy = to_rep(
        factor_all.at[chip_peer], factor_all.at[chip_peer], fa_send.at[5], fa_recv.at[5], core_peer
    )
    copy.start()
    small_copies.append(copy)

    size = slots // groups
    slot_copies = []
    for g in range(groups):

        def advance(j, carry, g=g):
            s = g * size + j
            found = owner_read[s]
            row = jnp.maximum(found - 1, 0)
            kept = jnp.full((momentum_all.shape[1], part), found, jnp.int32) > 0
            for q in range(4):
                at = pl.ds(q * part, part)
                moved = OUTER_MOMENTUM * momentum_all[s, :, at] + (
                    anchor_all[s, :, at] - gathered[q, row]
                )
                momentum_all[s, :, at] = jnp.where(kept, moved, 0.0)
            return carry

        lax.fori_loop(0, size, advance, 0)
        copy = pltpu.make_async_copy(
            momentum_all.at[pl.ds(g * size, size)],
            new_momentum.at[pl.ds(g * size, size)],
            slot_sem.at[g],
        )
        copy.start()
        slot_copies.append(copy)

    small_copies[6].wait_recv()
    small_copies[7].wait_recv()
    for q in range(4):
        copy = pltpu.make_async_copy(
            factor_all.at[q], factor_out.at[:, :, pl.ds(q * part, part)], factor_sem.at[q]
        )
        copy.start()
        tile_copies.append(copy)
    for copy in core_copies + [chip_copy] + held_copies + fresh_copies + small_copies:
        copy.wait_send()
    for copy in part_copies + group_copies:
        copy.wait_send()
    for k in range(own_count):
        if k:
            mean_copies[k].wait_send()
        near[k].wait_send()
        cross[k].wait_send()
        passed[k].wait_send()
    for copy in tile_copies + slot_copies:
        copy.wait()


def route(weights, anchor, momentum, embed, tables, own_count, per_pair):
    tiles, rows, width = weights.shape[1:]
    slots, part = anchor.shape[0], width // 4
    pairs = own_count * per_pair
    groups = 8 if slots % 8 == 0 else 1
    f32, dma = jnp.float32, pltpu.SemaphoreType.DMA
    scratch = [
        pltpu.VMEM((slots, rows, part), f32), pltpu.VMEM((slots, rows, part), f32),
        pltpu.VMEM((2, tiles, rows, part), f32), pltpu.VMEM((2, tiles, rows, part), f32),
        pltpu.VMEM((tiles, rows, part), f32), pltpu.VMEM((tiles, rows, part), f32),
        pltpu.VMEM((tiles, rows, part), f32),
        pltpu.VMEM((pairs, rows, part), f32), pltpu.VMEM((pairs, rows, part), f32),
        pltpu.VMEM((pairs, rows, part), f32), pltpu.VMEM((4, pairs, rows, part), f32),
        pltpu.VMEM((4, tiles, rows, part), f32),
        pltpu.VMEM((slots, rows, width), f32), pltpu.VMEM((slots, rows, width), f32),
        dma((6,)), dma((2,)), dma((2,)), dma((1,)), dma((1,)),
    ] + [dma((own_count,)) for _ in range(10)] + [dma((3,)), dma((3,)), dma((4,)), dma((groups,))]
    emb_rows, rank, chunks = embed[1].shape[0], embed[2].shape[0], 8
    chunk = (rank // chunks, part)
    scratch += [
        pltpu.VMEM((emb_rows, width), f32),
        pltpu.VMEM((rank, emb_rows), f32), pltpu.VMEM((rank, emb_rows), f32),
        pltpu.VMEM((rank, emb_rows), f32), pltpu.VMEM((rank, emb_rows), f32),
        pltpu.VMEM((4, chunks) + chunk, f32), pltpu.VMEM((2, chunks) + chunk, f32),
        pltpu.VMEM((chunks,) + chunk, f32), pltpu.VMEM((chunks,) + chunk, f32),
        pltpu.VMEM((chunks,) + chunk, f32), pltpu.VMEM((own_count,) + chunk, f32),
        pltpu.VMEM(chunk, f32), pltpu.VMEM((4, chunks) + chunk, f32),
        dma((2,)), dma((2,)), dma((6,)), dma((6,)), dma((own_count,)), dma((own_count,)),
        dma((chunks,)), dma((chunks,)), dma((4,)),
    ]
    return pl.pallas_call(
        functools.partial(route_kernel, own_count, per_pair, groups),
        out_shape=(
            jax.ShapeDtypeStruct((tiles, rows, width), f32),
            jax.ShapeDtypeStruct((slots, rows, width), f32),
            jax.ShapeDtypeStruct((chunks, rank // chunks, width), f32),
            jax.ShapeDtypeStruct((rank, emb_rows), f32),
        ),
        in_specs=[pl.BlockSpec(memory_space=pltpu.SMEM)] * 4 + [pl.BlockSpec(memory_space=pl.ANY)] * 3
        + [pl.BlockSpec(memory_space=pltpu.VMEM)] * 4,
        out_specs=(pl.BlockSpec(memory_space=pl.ANY),) * 3 + (pl.BlockSpec(memory_space=pltpu.VMEM),),
        scratch_shapes=scratch,
        compiler_params=pltpu.CompilerParams(
            collective_id=0, has_side_effects=True, vmem_limit_bytes=60 * 1024 * 1024
        ),
        cost_estimate=pl.CostEstimate(flops=20000000, bytes_accessed=300000000, transcendentals=0),
    )(*tables, weights, anchor, momentum, *embed)


def local(
    weights, anchor, momentum, owner, emb_weights, emb_anchor, emb_momentum, sketch, inv_root
):
    own_count = lax.axis_size("own")
    own_index = lax.axis_index("own")
    tiles_dev = weights.shape[1]
    capacity = anchor.shape[0]
    half_tiles = min(tiles_dev // 2, own_count)
    hot_count = max(own_count // 4, 1)
    per_pair = (tiles_dev - half_tiles) // hot_count + 1
    tables = owner_tables(owner, tiles_dev, per_pair, capacity, own_index, own_count)
    embed = (emb_weights, emb_anchor, sketch, inv_root)
    new_weights, new_momentum, factor, basis_rows = route(
        weights, anchor, momentum, embed, tables, own_count, per_pair
    )
    factor = factor.reshape(sketch.shape)
    highest = lax.Precision.HIGHEST
    approx = lax.dot_general(
        basis_rows,
        factor,
        (((0,), (0,)), ((), ())),
        precision=highest,
        preferred_element_type=jnp.float32,
    )
    new_emb_momentum = OUTER_MOMENTUM * emb_momentum + approx
    new_embedding = emb_anchor - OUTER_RATE * (approx + OUTER_MOMENTUM * new_emb_momentum)
    return (new_weights, new_momentum, new_embedding, new_emb_momentum)


def solution(mesh):
    placed = (
        P("rep", "own", None, None),
        P("own", None, None),
        P("own", None, None),
        P(),
        P("rep", "own", None),
        P("own", None),
        P("own", None),
        P(),
        P(),
    )
    return jax.shard_map(
        local,
        mesh=mesh,
        in_specs=placed,
        out_specs=(P("own", None, None), P("own", None, None), P("own", None), P("own", None)),
        check_vma=False,
    )
```
